256 devices in a mesh: mom: 4 (over x_hi, core), energy: 64 (over y, z, x_lo).
Axes of the slice: x: 4 (x_hi: 2, x_lo: 2; x = x_hi * 2 + x_lo), y: 4, z: 8, core: 2. Of those that a mesh axis runs over, the one named last changes fastest.
Arguments:
- green: float32 [512, 4, 24, 768], P('energy', 'mom'), may hold values from -6 to 6
- gradients: float32 [3, 12, 768], replicated, may hold values from -1.75 to 1.75
- neighbours: int32 [3, 64], replicated, may hold values from 0 to 63
- phonons: float32 [2, 3, 8, 4], replicated, may hold values from 0.02 to 0.2
- offsets: int32 [8], replicated, may hold values from 1 to 8, as said below
Outputs:
- sigma: float32 [512, 4, 24, 768], P('energy', 'mom')
The draws below stay inside these ranges and needn't reach their ends.
Inputs may be any that keep to these rules, and one draw needn't show every extreme that they name: `offsets`: some frequency takes exactly 8 energy steps.
All inputs are finite; a program needn't handle non-finite values.
Results may differ from the reference program's by a relative error of at most 0.0001.
Values sent between devices are 32-bit elements; how exact they have to be, the bound alone decides.
No kernel may reach another device: no remote copies, remote signals or barrier semaphores. Data moves between devices by JAX's collectives and lax.ppermute only.
A program may use at most 128 MiB of HBM per device.

```python
import math
import jax
import jax.numpy as jnp
from jax import lax

ORB = 12
NA = 64
DIRS = 3
NW = 8
HW = 8
NK = 4
NE = 512


def draw_offsets(key, part):
    first_key, second_key = jax.random.split(jax.random.fold_in(key, 11))
    values = jax.random.randint(first_key, (NW,), 1, HW + 1)
    where_top = jax.random.randint(second_key, (), 0, NW)
    return jnp.where(jnp.arange(NW) == where_top, HW, values).astype(jnp.int32)


def touch_ends(values, key, low, high):
    dims = values.shape
    place = [jax.random.randint(jax.random.fold_in(key, axis), (), 0, dims[axis]) for axis in range(len(dims))]
    values = values.at[tuple(place)].set(low)
    longest = dims.index(max(dims))
    place[longest] = (place[longest] + 1) % dims[longest]
    return values.at[tuple(place)].set(high)


def level_of(rng, extent, shards, smallest, high):
    level = 1.0
    for axis_at, blocks in shards:
        heights = jax.random.uniform(jax.random.fold_in(jax.random.fold_in(rng, 6), axis_at), (blocks,), jnp.float32, smallest / len(shards), high / len(shards))
        level = level * jnp.repeat(jnp.exp(heights), extent[axis_at] // blocks).reshape((-1,) + (1,) * (len(extent) - 1 - axis_at))
    return level


def noise(key, shape, deviation, bound, pieces=(), kind=jnp.bfloat16):
    array = deviation * jax.random.normal(key, shape, jnp.float32)
    if pieces:
        array = array * level_of(key, shape, pieces, -0.22, 0.18)
    return jnp.clip(array, -bound, bound).astype(kind)


def setup_inputs(seed: int = 0) -> dict:
    key_of = jax.random.split(jax.random.key(seed), 6)
    green = noise(key_of[0], (NE, NK, 2 * ORB, ORB * NA), 1.0, 6.0, ((0, 64), (1, 4)), jnp.float32)
    gradients = noise(key_of[1], (DIRS, ORB, ORB * NA), ORB ** -0.5, 1.75, (), jnp.float32)
    neighbours = touch_ends(jax.random.randint(key_of[2], (DIRS, NA), 0, NA), jax.random.fold_in(key_of[2], 1), 0, NA - 1).astype(jnp.int32)
    phonons = jnp.clip(jnp.exp(jax.random.uniform(key_of[3], (2, DIRS, NW, NK), jnp.float32, math.log(0.02), math.log(0.2))), 0.02, 0.2)
    offsets = draw_offsets(jax.random.fold_in(key_of[5], 71), 0)
    return {"green": green, "gradients": gradients, "neighbours": neighbours, "phonons": phonons, "offsets": offsets}


def sandwich(green, gradients, neighbours, direction):
    blocks = green.reshape(green.shape[0], green.shape[1], 2, ORB, ORB, NA)
    select = (neighbours[direction][None, :] == jnp.arange(NA, dtype=jnp.int32)[:, None]).astype(jnp.float32)
    picked = jnp.einsum('xkcijb,ba->xkcija', blocks, select, precision=lax.Precision.HIGHEST)
    coupling = gradients[direction].reshape(ORB, ORB, NA)
    left_side = jnp.einsum('pia,xkcija->xkcpja', coupling, picked, precision=lax.Precision.HIGHEST)
    result = jnp.einsum('xkcpja,qja->xkcpqa', left_side, coupling, precision=lax.Precision.HIGHEST)
    return result.reshape(green.shape)


def reference(green, gradients, neighbours, phonons, offsets):
    moments = jnp.arange(NK, dtype=jnp.int32)
    phonon_mom = (moments[:, None] - moments[None, :]) % NK
    total = jnp.zeros(green.shape, jnp.float32)
    for direction in range(DIRS):
        layers = sandwich(green, gradients, neighbours, direction)
        for freq in range(NW):
            for side in range(2):
                circle = phonons[side, direction, freq][phonon_mom]
                mixed = jnp.einsum('kl,elrf->ekrf', circle, layers, precision=lax.Precision.HIGHEST)
                shift_by = offsets[freq] if side == 0 else -offsets[freq]
                padded = jnp.pad(mixed, ((HW, HW), (0, 0), (0, 0), (0, 0)))
                part_sum = lax.dynamic_slice_in_dim(padded, (HW - shift_by).astype(jnp.int32), NE, 0)
                total = total + part_sum
    return total
```

```python
import functools

import jax
import jax.numpy as jnp
from jax import lax
from jax.experimental import pallas as pl
from jax.experimental.pallas import tpu as pltpu
from jax.sharding import PartitionSpec as P

ORB = 12
NA = 64
DIRS = 3
NW = 8
HW = 8
NK = 4
WIDTH = ORB * NA
PAIRS = WIDTH // 128

PARAMS = pltpu.CompilerParams(vmem_limit_bytes=24 * 1024 * 1024)


def split_kernel(green_ref, mine_ref, other_ref):
    half = lax.axis_index("mom") // 2
    for part in range(2):

        @pl.when(half == part)
        def _():
            for i in range(ORB):
                mine_ref[i] = green_ref[pl.ds(part * ORB + i, HW, stride=2 * ORB), :]
                other_ref[i] = green_ref[pl.ds((1 - part) * ORB + i, HW, stride=2 * ORB), :]


def prepare_kernel(phonons_ref, offsets_ref, gradients_ref, lhs_ref, left_ref, right_ref, rows_ref):
    low = lax.broadcasted_iota(jnp.int32, (ORB, 128), 1) < NA
    for d in range(DIRS):
        for jj in range(PAIRS):
            lanes = pl.ds(jj * 128, 128)
            rows = gradients_ref[d, :, lanes]
            swapped = pltpu.roll(rows, NA, 1)
            left_ref[2 * jj, d, pl.ds(0, ORB), :] = jnp.where(low, rows, swapped)
            left_ref[2 * jj + 1, d, pl.ds(0, ORB), :] = jnp.where(low, swapped, rows)
            rows_ref[pl.ds(0, ORB), :] = rows
            even = rows_ref[pl.ds(0, ORB // 2, stride=2), :]
            odd = rows_ref[pl.ds(1, ORB // 2, stride=2), :]
            first = low[: ORB // 2]
            right_ref[d, jj, 0, pl.ds(0, ORB // 2), :] = jnp.where(first, even, odd)
            right_ref[d, jj, 1, pl.ds(0, ORB // 2), :] = jnp.where(
                first, pltpu.roll(even, NA, 1), pltpu.roll(odd, NA, 1)
            )
    mom = lax.axis_index("mom")
    ahead = jnp.where(lax.axis_index("energy") % 2 == 0, HW, -HW)
    shape = (16, 256)
    row = lax.broadcasted_iota(jnp.int32, shape, 0)
    col = lax.broadcasted_iota(jnp.int32, shape, 1)
    edge = col < 128
    beyond = edge & (col % 64 >= 32)
    shift = jnp.where(edge, jnp.where(beyond, -ahead, ahead), 0)
    delta = row % 8 - col % 8 + shift
    target = mom ^ ((row // 8) * 2)
    source = mom ^ ((col // 8) % 4)
    circle = (target - source) & 3
    fresh = col % 128 < jnp.where(edge, 64, 32)
    for d in range(DIRS):
        total = jnp.zeros(shape, jnp.float32)
        for w in range(NW):
            offset = offsets_ref[w]
            for side in range(2):
                base = ((side * DIRS + d) * NW + w) * NK
                value = jnp.full(shape, phonons_ref[base], jnp.float32)
                for n in range(1, NK):
                    value = jnp.where(circle == n, phonons_ref[base + n], value)
                hit = delta == (offset if side == 0 else -offset)
                total = total + jnp.where(hit, value, 0.0)
        top = total.astype(jnp.bfloat16)
        rest = jnp.where(fresh, total - top.astype(jnp.float32), 0.0).astype(jnp.bfloat16)
        lhs_ref[pl.ds(d * 16, 16), :] = top
        lhs_ref[pl.ds(48 + d * 16, 16), :] = rest


def mix_kernel(count, first, *refs):
    sources = refs[:count]
    lhs_ref, left_ref, right_ref, pick_ref, own_ref, far_ref, mixed_ref, half_ref = refs[count:]
    outs = (own_ref, far_ref)
    depth = count * HW

    def mix(i, carry):
        block = jnp.concatenate([source[i] for source in sources], axis=0)
        top = block.astype(jnp.bfloat16)
        rest = (block - top.astype(jnp.float32)).astype(jnp.bfloat16)
        both = jnp.concatenate([top, rest], axis=0)
        product = jnp.dot(
            lhs_ref[:, first : first + 2 * depth], both, preferred_element_type=jnp.float32
        )
        mixed_ref[i] = product[:48] + product[48:]
        return carry

    lax.fori_loop(0, ORB, mix, 0)
    for d in range(DIRS):
        pick = pick_ref[pl.ds(d, HW, stride=0), :]

        def left_side(jj, carry):
            lanes = pl.ds(pl.multiple_of(jj * 128, 128), 128)
            picked = [
                [
                    jnp.take_along_axis(
                        mixed_ref[i, pl.ds(d * 16 + k * HW, HW), lanes],
                        pick,
                        axis=1,
                        mode="promise_in_bounds",
                    )
                    for i in range(ORB)
                ]
                for k in range(2)
            ]
            for p in range(ORB):
                sums = [None, None]
                for i in range(ORB):
                    factor = left_ref[i, d, pl.ds(p, HW, stride=0), :]
                    for k in range(2):
                        term = factor * picked[k][i]
                        sums[k] = term if sums[k] is None else sums[k] + term
                for k in range(2):
                    half_ref[k, p, :, lanes] = sums[k]
            return carry

        lax.fori_loop(0, PAIRS, left_side, 0)

        def right_side(p, carry):
            plain = [[half_ref[k, p, :, pl.ds(jj * 128, 128)] for jj in range(PAIRS)] for k in range(2)]
            swapped = [[pltpu.roll(v, NA, 1) for v in row] for row in plain]
            for q in range(PAIRS):
                sums = [None, None]
                for jj in range(PAIRS):
                    straight = right_ref[d, jj, 0, pl.ds(q, HW, stride=0), :]
                    crossed = right_ref[d, jj, 1, pl.ds(q, HW, stride=0), :]
                    for k in range(2):
                        term = straight * plain[k][jj] + crossed * swapped[k][jj]
                        sums[k] = term if sums[k] is None else sums[k] + term
                lanes = pl.ds(q * 128, 128)
                for k in range(2):
                    if d == 0:
                        outs[k][p, :, lanes] = sums[k]
                    else:
                        outs[k][p, :, lanes] += sums[k]
            return carry

        lax.fori_loop(0, ORB, right_side, 0)


def join_kernel(own_ref, far_ref, near_edge_ref, far_edge_ref, out_ref):
    half = lax.axis_index("mom") // 2
    for part in range(2):

        @pl.when(half == part)
        def _():
            for p in range(ORB):
                out_ref[pl.ds(part * ORB + p, HW, stride=2 * ORB), :] = own_ref[p] + near_edge_ref[p]
                out_ref[pl.ds((1 - part) * ORB + p, HW, stride=2 * ORB), :] = far_ref[p] + far_edge_ref[p]


def send(x, energy_of, flip):
    energies = lax.axis_size("energy")
    moms = lax.axis_size("mom")
    pairs = []
    for m in range(moms):
        for e in range(energies):
            to = energy_of(e)
            if 0 <= to < energies:
                pairs.append((m * energies + e, (m ^ flip) * energies + to))
    return lax.ppermute(x, ("mom", "energy"), pairs)


def stay(e):
    return e


def beyond(e):
    return e - 2 if e % 2 == 0 else e + 2


def pair(e):
    return e ^ 1


VMEM = pl.BlockSpec(memory_space=pltpu.VMEM)
SMEM = pl.BlockSpec(memory_space=pltpu.SMEM)
FLAT_LANES = pl.BlockSpec((HW * 2 * ORB, 128), lambda j: (0, j))
BLOCK_LANES = pl.BlockSpec((ORB, HW, 128), lambda j: (0, 0, j))
BLOCK = jax.ShapeDtypeStruct((ORB, HW, WIDTH), jnp.float32)


def mix_call(sources, lhs, left, right, pick, first):
    count = len(sources)
    return pl.pallas_call(
        functools.partial(mix_kernel, count, first),
        out_shape=(BLOCK, BLOCK),
        in_specs=[VMEM] * (count + 4),
        out_specs=(VMEM, VMEM),
        scratch_shapes=[
            pltpu.VMEM((ORB, 48, WIDTH), jnp.float32),
            pltpu.VMEM((2, ORB, HW, WIDTH), jnp.float32),
        ],
        compiler_params=PARAMS,
        name="mix",
    )(*sources, lhs, left, right, pick)


def per_device(green, gradients, neighbours, phonons, offsets):
    mine, other = pl.pallas_call(
        split_kernel,
        out_shape=(BLOCK, BLOCK),
        grid=(PAIRS,),
        in_specs=[FLAT_LANES],
        out_specs=(BLOCK_LANES, BLOCK_LANES),
        compiler_params=PARAMS,
        name="split",
    )(green.reshape(HW * 2 * ORB, WIDTH))
    beyond_far = send(other, beyond, 2)
    beyond_own = send(mine, beyond, 0)
    here_far = send(other, stay, 2)
    here_near = send(mine, stay, 1)
    here_last = send(here_far, stay, 1)
    beyond_near = send(beyond_own, stay, 1)
    beyond_last = send(beyond_far, stay, 1)
    lhs, left, right = pl.pallas_call(
        prepare_kernel,
        out_shape=(
            jax.ShapeDtypeStruct((96, 256), jnp.bfloat16),
            jax.ShapeDtypeStruct((ORB, DIRS, 16, 128), jnp.float32),
            jax.ShapeDtypeStruct((DIRS, PAIRS, 2, 8, 128), jnp.float32),
        ),
        in_specs=[SMEM, SMEM, VMEM],
        out_specs=(VMEM, VMEM, VMEM),
        scratch_shapes=[pltpu.VMEM((16, 128), jnp.float32)],
        compiler_params=PARAMS,
        name="prepare",
    )(phonons.reshape(-1), offsets, gradients)
    pick = jnp.concatenate([neighbours, neighbours + NA], axis=1)
    here = [mine, here_near, here_far, here_last]
    there = [beyond_own, beyond_near, beyond_far, beyond_last]
    own, far = mix_call(here, lhs, left, right, pick, 128)
    far = send(far, stay, 2)
    near_edge, far_edge = mix_call(here + there, lhs, left, right, pick, 0)
    near_edge = send(near_edge, pair, 0)
    far_edge = send(far_edge, pair, 2)
    out = pl.pallas_call(
        join_kernel,
        out_shape=jax.ShapeDtypeStruct((HW * 2 * ORB, WIDTH), jnp.float32),
        grid=(PAIRS,),
        in_specs=[BLOCK_LANES] * 4,
        out_specs=FLAT_LANES,
        compiler_params=PARAMS,
        name="join",
    )(own, far, near_edge, far_edge)
    return out.reshape(green.shape)


def solution(mesh):
    placed = (P("energy", "mom", None, None), P(), P(), P(), P())
    return jax.shard_map(
        per_device,
        mesh=mesh,
        in_specs=placed,
        out_specs=P("energy", "mom", None, None),
        check_vma=False,
    )
```

```python
import functools

import jax
import jax.numpy as jnp
from jax import lax
from jax.experimental import pallas as pl
from jax.experimental.pallas import tpu as pltpu
from jax.sharding import PartitionSpec as P


ORB = 12
NA = 64
DIRS = 3
NW = 8
HW = 8
NK = 4
WIDTH = ORB * NA
PAIRS = WIDTH // 128
UNROLL_RIGHT = 2
GROUP = 4 * HW

PARAMS = pltpu.CompilerParams(vmem_limit_bytes=24 * 1024 * 1024)


def split_kernel(green_ref, mine_ref, other_ref, staged_ref, sems):
    half = lax.axis_index("mom") // 2

    def fetch(j):
        lanes = pl.ds(j * 128, 128)
        return pltpu.make_async_copy(green_ref.at[:, lanes], staged_ref.at[j], sems.at[j])

    for j in range(PAIRS):
        fetch(j).start()
    for j in range(PAIRS):
        fetch(j).wait()
        lanes = pl.ds(j * 128, 128)
        for part in range(2):

            @pl.when(half == part)
            def _():
                for i in range(ORB):
                    mine_ref[i, :, lanes] = staged_ref[j, pl.ds(part * ORB + i, HW, stride=2 * ORB), :]
                    other_ref[i, :, lanes] = staged_ref[
                        j, pl.ds((1 - part) * ORB + i, HW, stride=2 * ORB), :
                    ]


def prepare_kernel(
    phonons_ref, offsets_ref, neighbours_ref, gradients_ref, lhs_ref, left_ref, right_ref, pick_ref, rows_ref
):
    pick_ref[pl.ds(0, DIRS), pl.ds(0, NA)] = neighbours_ref[...]
    pick_ref[pl.ds(0, DIRS), pl.ds(NA, NA)] = neighbours_ref[...] + NA
    low = lax.broadcasted_iota(jnp.int32, (ORB, 128), 1) < NA
    for d in range(DIRS):
        for jj in range(PAIRS):
            lanes = pl.ds(jj * 128, 128)
            rows = gradients_ref[d, :, lanes]
            swapped = pltpu.roll(rows, NA, 1)
            left_ref[2 * jj, d, pl.ds(0, ORB), :] = jnp.where(low, rows, swapped)
            left_ref[2 * jj + 1, d, pl.ds(0, ORB), :] = jnp.where(low, swapped, rows)
            rows_ref[pl.ds(0, ORB), :] = rows
            even = rows_ref[pl.ds(0, ORB // 2, stride=2), :]
            odd = rows_ref[pl.ds(1, ORB // 2, stride=2), :]
            first = low[: ORB // 2]
            right_ref[d, jj, 0, pl.ds(0, ORB // 2), :] = jnp.where(first, even, odd)
            right_ref[d, jj, 1, pl.ds(0, ORB // 2), :] = jnp.where(
                first, pltpu.roll(even, NA, 1), pltpu.roll(odd, NA, 1)
            )
    mom = lax.axis_index("mom")
    ahead = jnp.where(lax.axis_index("energy") % 2 == 0, HW, -HW)
    shape = (HW, 384)
    row = lax.broadcasted_iota(jnp.int32, shape, 0)
    col = lax.broadcasted_iota(jnp.int32, shape, 1)
    edge = col < 256
    there = edge & (col % 64 >= 32)
    shift = jnp.where(edge, jnp.where(there, -ahead, ahead), 0)
    delta = row - col % 8 + shift
    source = mom ^ ((col // 8) % 4)
    depth = jnp.where(edge, 64, 32)
    fine = col % 256 >= 2 * depth
    for k in range(2):
        circle = ((mom ^ (2 * k)) - source) & 3
        blocks = []
        for d in range(DIRS):
            total = jnp.zeros(shape, jnp.float32)
            for w in range(NW):
                offset = offsets_ref[w]
                for side in range(2):
                    value = jnp.full(shape, phonons_ref[side, d, 0, w], jnp.float32)
                    for n in range(1, NK):
                        value = jnp.where(circle == n, phonons_ref[side, d, n, w], value)
                    hit = delta == (offset if side == 0 else -offset)
                    total = total + jnp.where(hit, value, 0.0)
            top = total.astype(jnp.bfloat16).astype(jnp.float32)
            blocks.append(jnp.where(fine, total - top, top))
        blocks.append(jnp.zeros(shape, jnp.float32))
        lhs_ref[pl.ds(k * GROUP, GROUP), :] = jnp.concatenate(blocks, axis=0).astype(jnp.bfloat16)


def left_products(picked, left_ref, half_ref, d, k, start, lanes):
    for p in range(half_ref.shape[2]):
        total = None
        for i in range(ORB):
            term = left_ref[i, d, pl.ds(start + p, HW, stride=0), :] * picked[i]
            total = term if total is None else total + term
        half_ref[d, k, p, 0, :, lanes] = total
        half_ref[d, k, p, 1, :, lanes] = pltpu.roll(total, NA, 1)


def right_products(right_ref, half_ref, outs):
    for k, out_ref in enumerate(outs):

        def right_side(p, carry):
            sums = [None] * PAIRS
            for d in range(DIRS):
                plain, swapped = (
                    [half_ref[d, k, p, n, :, pl.ds(jj * 128, 128)] for jj in range(PAIRS)] for n in range(2)
                )
                for q in range(PAIRS):
                    for jj in range(PAIRS):
                        straight = right_ref[d, jj, 0, pl.ds(q, HW, stride=0), :]
                        crossed = right_ref[d, jj, 1, pl.ds(q, HW, stride=0), :]
                        term = straight * plain[jj] + crossed * swapped[jj]
                        sums[q] = term if sums[q] is None else sums[q] + term
            for q in range(PAIRS):
                out_ref[p, :, pl.ds(q * 128, 128)] = sums[q]
            return carry

        lax.fori_loop(0, out_ref.shape[0], right_side, 0, unroll=UNROLL_RIGHT)


def mix_kernel(count, first, moms, keep, *refs):
    sources = refs[:count]
    lhs_ref, left_ref, right_ref, pick_ref, *outs = refs[count:-2]
    mixed_ref, half_ref = refs[-2:]
    kept_ref = outs.pop() if keep else None
    depth = count * HW
    rows = len(moms) * GROUP

    def mix(jj, slot):
        lanes = pl.ds(pl.multiple_of(jj * 128, 128), 128)
        weights = lhs_ref[pl.ds(moms[0] * GROUP, rows), first : first + 3 * depth]
        for i in range(0, ORB, 2):
            block = jnp.concatenate(
                [
                    jnp.concatenate([source[i + n, :, lanes] for source in sources], axis=0)
                    for n in range(2)
                ],
                axis=1,
            )
            top = block.astype(jnp.bfloat16)
            rest = (block - top.astype(jnp.float32)).astype(jnp.bfloat16)
            product = jnp.dot(
                weights,
                jnp.concatenate([top, rest, top], axis=0),
                preferred_element_type=jnp.float32,
            )
            for k in range(len(moms)):
                for d in range(DIRS):
                    at = k * GROUP + d * HW
                    total = product[at : at + HW]
                    mixed_ref[slot, i, k, d] = total[:, :128]
                    mixed_ref[slot, i + 1, k, d] = total[:, 128:]

    def left_side(jj, slot):
        lanes = pl.ds(pl.multiple_of(jj * 128, 128), 128)
        for d in range(DIRS):
            pick = pick_ref[pl.ds(d, HW, stride=0), :]
            for k in range(len(moms)):
                picked = [
                    jnp.take_along_axis(
                        mixed_ref[slot, i, k, d], pick, axis=1, mode="promise_in_bounds"
                    )
                    for i in range(ORB)
                ]
                if keep:
                    for i in range(ORB):
                        kept_ref[jj, d, k, i] = picked[i]
                left_products(picked, left_ref, half_ref, d, k, 0, lanes)

    mix(0, 0)

    def step(t, carry):
        mix(2 * t + 1, 1)
        left_side(2 * t, 0)
        mix(jnp.minimum(2 * t + 2, PAIRS - 1), 0)
        left_side(2 * t + 1, 1)
        return carry

    lax.fori_loop(0, PAIRS // 2, step, 0)
    right_products(right_ref, half_ref, outs)


def join_kernel(own_ref, far_ref, near_edge_ref, far_edge_ref, out_ref, staged_ref, sems):
    half = lax.axis_index("mom") // 2

    def flush(j):
        lanes = pl.ds(j * 128, 128)
        return pltpu.make_async_copy(staged_ref.at[j], out_ref.at[:, lanes], sems.at[j])

    for j in range(PAIRS):
        lanes = pl.ds(j * 128, 128)
        for part in range(2):

            @pl.when(half == part)
            def _():
                for p in range(ORB):
                    staged_ref[j, pl.ds(part * ORB + p, HW, stride=2 * ORB), :] = (
                        own_ref[p, :, lanes] + near_edge_ref[p, :, lanes]
                    )
                    staged_ref[j, pl.ds((1 - part) * ORB + p, HW, stride=2 * ORB), :] = (
                        far_ref[p, :, lanes] + far_edge_ref[p, :, lanes]
                    )

        flush(j).start()
    for j in range(PAIRS):
        flush(j).wait()


def send(x, energy_of, flip):
    energies = lax.axis_size("energy")
    moms = lax.axis_size("mom")
    pairs = []
    for m in range(moms):
        for e in range(energies):
            to = energy_of(e)
            if 0 <= to < energies:
                pairs.append((m * energies + e, (m ^ flip) * energies + to))
    return lax.ppermute(x, ("mom", "energy"), pairs)


def stay(e):
    return e


def beyond(e):
    return e - 2 if e % 2 == 0 else e + 2


def pair(e):
    return e ^ 1


VMEM = pl.BlockSpec(memory_space=pltpu.VMEM)
SMEM = pl.BlockSpec(memory_space=pltpu.SMEM)
HBM = pl.BlockSpec(memory_space=pltpu.MemorySpace.HBM)
STAGED = [pltpu.VMEM((PAIRS, HW * 2 * ORB, 128), jnp.float32), pltpu.SemaphoreType.DMA((PAIRS,))]
BLOCK = jax.ShapeDtypeStruct((ORB, HW, WIDTH), jnp.float32)


def mix_call(sources, tables, first, moms, orbitals, keep=False):
    count = len(sources)
    outs = [jax.ShapeDtypeStruct((orbitals, HW, WIDTH), jnp.float32)] * len(moms)
    if keep:
        outs.append(jax.ShapeDtypeStruct((PAIRS, DIRS, len(moms), ORB, HW, 128), jnp.float32))
    return pl.pallas_call(
        functools.partial(mix_kernel, count, first, moms, keep),
        out_shape=tuple(outs),
        in_specs=[VMEM] * (count + 4),
        out_specs=(VMEM,) * len(outs),
        scratch_shapes=[
            pltpu.VMEM((2, ORB, len(moms), DIRS, HW, 128), jnp.float32),
            pltpu.VMEM((DIRS, len(moms), orbitals, 2, HW, WIDTH), jnp.float32),
        ],
        compiler_params=PARAMS,
        name="mix",
    )(*sources, *tables)


def layer(green, gradients, neighbours, phonons, offsets):
    mine, other = pl.pallas_call(
        split_kernel,
        out_shape=(BLOCK, BLOCK),
        in_specs=[HBM],
        out_specs=(VMEM, VMEM),
        scratch_shapes=STAGED,
        compiler_params=PARAMS,
        name="split",
    )(green.reshape(HW * 2 * ORB, WIDTH))
    here_far = send(other, stay, 2)
    beyond_own = send(mine, beyond, 0)
    here_near = send(mine, stay, 1)
    tables = pl.pallas_call(
        prepare_kernel,
        out_shape=(
            jax.ShapeDtypeStruct((2 * GROUP, 384), jnp.bfloat16),
            jax.ShapeDtypeStruct((ORB, DIRS, 16, 128), jnp.float32),
            jax.ShapeDtypeStruct((DIRS, PAIRS, 2, 8, 128), jnp.float32),
            jax.ShapeDtypeStruct((8, 128), jnp.int32),
        ),
        in_specs=[SMEM, SMEM, VMEM, VMEM],
        out_specs=(VMEM,) * 4,
        scratch_shapes=[pltpu.VMEM((16, 128), jnp.float32)],
        compiler_params=PARAMS,
        name="prepare",
    )(phonons.transpose(0, 1, 3, 2), offsets, neighbours, gradients)
    here_far, *tables = lax.optimization_barrier((here_far, *tables))
    beyond_far = send(here_far, beyond, 0)
    here_last = send(here_far, stay, 1)
    here = [mine, here_near, here_far, here_last]
    (far,) = mix_call(here, tables, 256, (1,), ORB)
    _, beyond_own, beyond_far = lax.optimization_barrier((far, beyond_own, beyond_far))
    far = send(far, stay, 2)
    there = [beyond_own, send(beyond_own, stay, 1), beyond_far, send(beyond_far, stay, 1)]
    near_edge, far_edge = mix_call(here + there, tables, 0, (0, 1), ORB)
    edges = [send(near_edge, pair, 0), send(far_edge, pair, 2)]
    here[0], near_edge = lax.optimization_barrier((mine, near_edge))
    (own,) = mix_call(here, tables, 256, (0,), ORB)
    out = pl.pallas_call(
        join_kernel,
        out_shape=jax.ShapeDtypeStruct((HW * 2 * ORB, WIDTH), jnp.float32),
        in_specs=[VMEM] * 4,
        out_specs=HBM,
        scratch_shapes=STAGED,
        compiler_params=PARAMS,
        name="join",
    )(own, far, *edges)
    return out.reshape(green.shape)


def solution(mesh):
    placed = (P("energy", "mom", None, None), P(), P(), P(), P())
    return jax.shard_map(
        layer,
        mesh=mesh,
        in_specs=placed,
        out_specs=P("energy", "mom", None, None),
        check_vma=False,
    )
```

```python
import functools

import jax
import jax.numpy as jnp
from jax import lax
from jax.experimental import pallas as pl
from jax.experimental.pallas import tpu as pltpu
from jax.sharding import PartitionSpec as P


ORB = 12
NA = 64
DIRS = 3
NW = 8
HW = 8
NK = 4
WIDTH = ORB * NA
PAIRS = WIDTH // 128
UNROLL_RIGHT = 6
GROUP = 4 * HW

PARAMS = pltpu.CompilerParams(vmem_limit_bytes=24 * 1024 * 1024)


def split_kernel(green_ref, mine_ref, other_ref, staged_ref, sems):
    half = lax.axis_index("mom") // 2

    def fetch(j):
        lanes = pl.ds(j * 128, 128)
        return pltpu.make_async_copy(green_ref.at[:, lanes], staged_ref.at[j], sems.at[j])

    for j in range(PAIRS):
        fetch(j).start()
    for j in range(PAIRS):
        fetch(j).wait()
        lanes = pl.ds(j * 128, 128)
        for part in range(2):

            @pl.when(half == part)
            def _():
                for i in range(ORB):
                    mine_ref[i, :, lanes] = staged_ref[j, pl.ds(part * ORB + i, HW, stride=2 * ORB), :]
                    other_ref[i, :, lanes] = staged_ref[
                        j, pl.ds((1 - part) * ORB + i, HW, stride=2 * ORB), :
                    ]


def prepare_kernel(
    phonons_ref, offsets_ref, neighbours_ref, gradients_ref, lhs_ref, left_ref, right_ref, pick_ref, rows_ref
):
    pick_ref[pl.ds(0, DIRS), pl.ds(0, NA)] = neighbours_ref[...]
    pick_ref[pl.ds(0, DIRS), pl.ds(NA, NA)] = neighbours_ref[...] + NA
    low = lax.broadcasted_iota(jnp.int32, (ORB, 128), 1) < NA
    for d in range(DIRS):
        for jj in range(PAIRS):
            lanes = pl.ds(jj * 128, 128)
            rows = gradients_ref[d, :, lanes]
            swapped = pltpu.roll(rows, NA, 1)
            left_ref[2 * jj, d, pl.ds(0, ORB), :] = jnp.where(low, rows, swapped)
            left_ref[2 * jj + 1, d, pl.ds(0, ORB), :] = jnp.where(low, swapped, rows)
            rows_ref[pl.ds(0, ORB), :] = rows
            even = rows_ref[pl.ds(0, ORB // 2, stride=2), :]
            odd = rows_ref[pl.ds(1, ORB // 2, stride=2), :]
            first = low[: ORB // 2]
            right_ref[d, jj, 0, pl.ds(0, ORB // 2), :] = jnp.where(first, even, odd)
            right_ref[d, jj, 1, pl.ds(0, ORB // 2), :] = jnp.where(
                first, pltpu.roll(even, NA, 1), pltpu.roll(odd, NA, 1)
            )
    mom = lax.axis_index("mom")
    ahead = jnp.where(lax.axis_index("energy") % 2 == 0, HW, -HW)
    shape = (HW, 384)
    row = lax.broadcasted_iota(jnp.int32, shape, 0)
    col = lax.broadcasted_iota(jnp.int32, shape, 1)
    edge = col < 256
    there = edge & (col % 64 >= 32)
    shift = jnp.where(edge, jnp.where(there, -ahead, ahead), 0)
    delta = row - col % 8 + shift
    source = mom ^ ((col // 8) % 4)
    depth = jnp.where(edge, 64, 32)
    fine = col % 256 >= 2 * depth
    for k in range(2):
        circle = ((mom ^ (2 * k)) - source) & 3
        blocks = []
        for d in range(DIRS):
            total = jnp.zeros(shape, jnp.float32)
            for w in range(NW):
                offset = offsets_ref[w]
                for side in range(2):
                    value = jnp.full(shape, phonons_ref[side, d, 0, w], jnp.float32)
                    for n in range(1, NK):
                        value = jnp.where(circle == n, phonons_ref[side, d, n, w], value)
                    hit = delta == (offset if side == 0 else -offset)
                    total = total + jnp.where(hit, value, 0.0)
            top = total.astype(jnp.bfloat16).astype(jnp.float32)
            blocks.append(jnp.where(fine, total - top, top))
        blocks.append(jnp.zeros(shape, jnp.float32))
        lhs_ref[pl.ds(k * GROUP, GROUP), :] = jnp.concatenate(blocks, axis=0).astype(jnp.bfloat16)


def left_products(picked, left_ref, half_ref, d, k, start, lanes):
    for p in range(half_ref.shape[2]):
        total = None
        for i in range(ORB):
            term = left_ref[i, d, pl.ds(start + p, HW, stride=0), :] * picked[i]
            total = term if total is None else total + term
        half_ref[d, k, p, :, lanes] = total


def right_products(right_ref, half_ref, outs):
    for k, out_ref in enumerate(outs):

        def right_side(p, carry):
            sums = [None] * PAIRS
            for d in range(DIRS):
                plain = [half_ref[d, k, p, :, pl.ds(jj * 128, 128)] for jj in range(PAIRS)]
                swapped = [pltpu.roll(v, NA, 1) for v in plain]
                for q in range(PAIRS):
                    for jj in range(PAIRS):
                        straight = right_ref[d, jj, 0, pl.ds(q, HW, stride=0), :]
                        crossed = right_ref[d, jj, 1, pl.ds(q, HW, stride=0), :]
                        term = straight * plain[jj] + crossed * swapped[jj]
                        sums[q] = term if sums[q] is None else sums[q] + term
            for q in range(PAIRS):
                out_ref[p, :, pl.ds(q * 128, 128)] = sums[q]
            return carry

        lax.fori_loop(0, out_ref.shape[0], right_side, 0, unroll=UNROLL_RIGHT)


def mix_kernel(count, first, moms, *refs):
    sources = refs[:count]
    lhs_ref, left_ref, right_ref, pick_ref, *outs = refs[count:-2]
    mixed_ref, half_ref = refs[-2:]
    depth = count * HW
    rows = len(moms) * GROUP

    def mix(jj, slot):
        lanes = pl.ds(pl.multiple_of(jj * 128, 128), 128)
        weights = lhs_ref[pl.ds(moms[0] * GROUP, rows), first : first + 3 * depth]
        for i in range(0, ORB, 2):
            block = jnp.concatenate(
                [
                    jnp.concatenate([source[i + n, :, lanes] for source in sources], axis=0)
                    for n in range(2)
                ],
                axis=1,
            )
            top = block.astype(jnp.bfloat16)
            rest = (block - top.astype(jnp.float32)).astype(jnp.bfloat16)
            product = jnp.dot(
                weights,
                jnp.concatenate([top, rest, top], axis=0),
                preferred_element_type=jnp.float32,
            )
            for k in range(len(moms)):
                for d in range(DIRS):
                    at = k * GROUP + d * HW
                    total = product[at : at + HW]
                    mixed_ref[slot, i, k, d] = total[:, :128]
                    mixed_ref[slot, i + 1, k, d] = total[:, 128:]

    def left_side(jj, slot):
        lanes = pl.ds(pl.multiple_of(jj * 128, 128), 128)
        for d in range(DIRS):
            pick = pick_ref[pl.ds(d, HW, stride=0), :]
            for k in range(len(moms)):
                picked = [
                    jnp.take_along_axis(
                        mixed_ref[slot, i, k, d], pick, axis=1, mode="promise_in_bounds"
                    )
                    for i in range(ORB)
                ]
                left_products(picked, left_ref, half_ref, d, k, 0, lanes)

    mix(0, 0)

    def step(t, carry):
        mix(2 * t + 1, 1)
        left_side(2 * t, 0)
        mix(jnp.minimum(2 * t + 2, PAIRS - 1), 0)
        left_side(2 * t + 1, 1)
        return carry

    lax.fori_loop(0, PAIRS // 2, step, 0)
    right_products(right_ref, half_ref, outs)


def join_kernel(own_ref, far_ref, near_edge_ref, far_edge_ref, out_ref, staged_ref, sems):
    half = lax.axis_index("mom") // 2

    def flush(j):
        lanes = pl.ds(j * 128, 128)
        return pltpu.make_async_copy(staged_ref.at[j], out_ref.at[:, lanes], sems.at[j])

    for j in range(PAIRS):
        lanes = pl.ds(j * 128, 128)
        for part in range(2):

            @pl.when(half == part)
            def _():
                for p in range(ORB):
                    staged_ref[j, pl.ds(part * ORB + p, HW, stride=2 * ORB), :] = (
                        own_ref[p, :, lanes] + near_edge_ref[p, :, lanes]
                    )
                    staged_ref[j, pl.ds((1 - part) * ORB + p, HW, stride=2 * ORB), :] = (
                        far_ref[p, :, lanes] + far_edge_ref[p, :, lanes]
                    )

        flush(j).start()
    for j in range(PAIRS):
        flush(j).wait()


def send(x, energy_of, flip):
    energies = lax.axis_size("energy")
    moms = lax.axis_size("mom")
    pairs = []
    for m in range(moms):
        for e in range(energies):
            to = energy_of(e)
            if 0 <= to < energies:
                pairs.append((m * energies + e, (m ^ flip) * energies + to))
    return lax.ppermute(x, ("mom", "energy"), pairs)


def stay(e):
    return e


def beyond(e):
    return e - 2 if e % 2 == 0 else e + 2


def pair(e):
    return e ^ 1


VMEM = pl.BlockSpec(memory_space=pltpu.VMEM)
SMEM = pl.BlockSpec(memory_space=pltpu.SMEM)
HBM = pl.BlockSpec(memory_space=pltpu.MemorySpace.HBM)
STAGED = [pltpu.VMEM((PAIRS, HW * 2 * ORB, 128), jnp.float32), pltpu.SemaphoreType.DMA((PAIRS,))]
BLOCK = jax.ShapeDtypeStruct((ORB, HW, WIDTH), jnp.float32)


def mix_call(sources, tables, first, moms, orbitals):
    count = len(sources)
    outs = [jax.ShapeDtypeStruct((orbitals, HW, WIDTH), jnp.float32)] * len(moms)
    return pl.pallas_call(
        functools.partial(mix_kernel, count, first, moms),
        out_shape=tuple(outs),
        in_specs=[VMEM] * (count + 4),
        out_specs=(VMEM,) * len(outs),
        scratch_shapes=[
            pltpu.VMEM((2, ORB, len(moms), DIRS, HW, 128), jnp.float32),
            pltpu.VMEM((DIRS, len(moms), orbitals, HW, WIDTH), jnp.float32),
        ],
        compiler_params=PARAMS,
        name="mix",
    )(*sources, *tables)


def layer(green, gradients, neighbours, phonons, offsets):
    mine, other = pl.pallas_call(
        split_kernel,
        out_shape=(BLOCK, BLOCK),
        in_specs=[HBM],
        out_specs=(VMEM, VMEM),
        scratch_shapes=STAGED,
        compiler_params=PARAMS,
        name="split",
    )(pltpu.with_memory_space_constraint(green.reshape(HW * 2 * ORB, WIDTH), pltpu.MemorySpace.HBM))
    here_far = send(other, stay, 2)
    beyond_own = send(mine, beyond, 0)
    here_near = send(mine, stay, 1)
    tables = pl.pallas_call(
        prepare_kernel,
        out_shape=(
            jax.ShapeDtypeStruct((2 * GROUP, 384), jnp.bfloat16),
            jax.ShapeDtypeStruct((ORB, DIRS, 16, 128), jnp.float32),
            jax.ShapeDtypeStruct((DIRS, PAIRS, 2, 8, 128), jnp.float32),
            jax.ShapeDtypeStruct((8, 128), jnp.int32),
        ),
        in_specs=[SMEM, SMEM, VMEM, VMEM],
        out_specs=(VMEM,) * 4,
        scratch_shapes=[pltpu.VMEM((16, 128), jnp.float32)],
        compiler_params=PARAMS,
        name="prepare",
    )(phonons.transpose(0, 1, 3, 2), offsets, neighbours, gradients)
    here_far, *tables = lax.optimization_barrier((here_far, *tables))
    beyond_far = send(here_far, beyond, 0)
    here_last = send(here_far, stay, 1)
    here = [mine, here_near, here_far, here_last]
    (far,) = mix_call(here, tables, 256, (1,), ORB)
    _, beyond_own, beyond_far = lax.optimization_barrier((far, beyond_own, beyond_far))
    far = send(far, stay, 2)
    there = [beyond_own, send(beyond_own, stay, 1), beyond_far, send(beyond_far, stay, 1)]
    near_edge, far_edge = mix_call(here + there, tables, 0, (0, 1), ORB)
    edges = [send(near_edge, pair, 0), send(far_edge, pair, 2)]
    here[0], near_edge = lax.optimization_barrier((mine, near_edge))
    (own,) = mix_call(here, tables, 256, (0,), ORB)
    out = pl.pallas_call(
        join_kernel,
        out_shape=jax.ShapeDtypeStruct((HW * 2 * ORB, WIDTH), jnp.float32),
        in_specs=[VMEM] * 4,
        out_specs=HBM,
        scratch_shapes=STAGED,
        compiler_params=PARAMS,
        name="join",
    )(own, far, *edges)
    return out.reshape(green.shape)


def solution(mesh):
    placed = (P("energy", "mom", None, None), P(), P(), P(), P())
    return jax.shard_map(
        layer,
        mesh=mesh,
        in_specs=placed,
        out_specs=P("energy", "mom", None, None),
        check_vma=False,
    )
```

```python
import functools

import jax
import jax.numpy as jnp
from jax import lax
from jax.experimental import pallas as pl
from jax.experimental.pallas import tpu as pltpu
from jax.sharding import PartitionSpec as P


ORB = 12
NA = 64
DIRS = 3
NW = 8
HW = 8
NK = 4
WIDTH = ORB * NA
PAIRS = WIDTH // 128
UNROLL_RIGHT = 12
GROUP = 4 * HW

PARAMS = pltpu.CompilerParams(vmem_limit_bytes=24 * 1024 * 1024)


def split_kernel(green_ref, mine_ref, other_ref, staged_ref, sems):
    half = lax.axis_index("mom") // 2

    def fetch(j):
        lanes = pl.ds(j * 128, 128)
        return pltpu.make_async_copy(green_ref.at[:, lanes], staged_ref.at[j], sems.at[j])

    for j in range(PAIRS):
        fetch(j).start()
    for j in range(PAIRS):
        fetch(j).wait()
        lanes = pl.ds(j * 128, 128)
        for part in range(2):

            @pl.when(half == part)
            def _():
                for i in range(ORB):
                    mine_ref[i, :, lanes] = staged_ref[j, pl.ds(part * ORB + i, HW, stride=2 * ORB), :]
                    other_ref[i, :, lanes] = staged_ref[
                        j, pl.ds((1 - part) * ORB + i, HW, stride=2 * ORB), :
                    ]


def prepare_kernel(
    phonons_ref, offsets_ref, neighbours_ref, gradients_ref, lhs_ref, left_ref, right_ref, pick_ref, rows_ref
):
    pick_ref[pl.ds(0, DIRS), pl.ds(0, NA)] = neighbours_ref[...]
    pick_ref[pl.ds(0, DIRS), pl.ds(NA, NA)] = neighbours_ref[...] + NA
    low = lax.broadcasted_iota(jnp.int32, (ORB, 128), 1) < NA
    for d in range(DIRS):
        for jj in range(PAIRS):
            lanes = pl.ds(jj * 128, 128)
            rows = gradients_ref[d, :, lanes]
            swapped = pltpu.roll(rows, NA, 1)
            left_ref[2 * jj, d, pl.ds(0, ORB), :] = jnp.where(low, rows, swapped)
            left_ref[2 * jj + 1, d, pl.ds(0, ORB), :] = jnp.where(low, swapped, rows)
            rows_ref[pl.ds(0, ORB), :] = rows
            even = rows_ref[pl.ds(0, ORB // 2, stride=2), :]
            odd = rows_ref[pl.ds(1, ORB // 2, stride=2), :]
            first = low[: ORB // 2]
            right_ref[d, jj, 0, pl.ds(0, ORB // 2), :] = jnp.where(first, even, odd)
            right_ref[d, jj, 1, pl.ds(0, ORB // 2), :] = jnp.where(
                first, pltpu.roll(even, NA, 1), pltpu.roll(odd, NA, 1)
            )
    mom = lax.axis_index("mom")
    ahead = jnp.where(lax.axis_index("energy") % 2 == 0, HW, -HW)
    shape = (HW, 384)
    row = lax.broadcasted_iota(jnp.int32, shape, 0)
    col = lax.broadcasted_iota(jnp.int32, shape, 1)
    edge = col < 256
    there = edge & (col % 64 >= 32)
    shift = jnp.where(edge, jnp.where(there, -ahead, ahead), 0)
    delta = row - col % 8 + shift
    source = mom ^ ((col // 8) % 4)
    depth = jnp.where(edge, 64, 32)
    fine = col % 256 >= 2 * depth
    for k in range(2):
        circle = ((mom ^ (2 * k)) - source) & 3
        blocks = []
        for d in range(DIRS):
            total = jnp.zeros(shape, jnp.float32)
            for w in range(NW):
                offset = offsets_ref[w]
                for side in range(2):
                    value = jnp.full(shape, phonons_ref[side, d, 0, w], jnp.float32)
                    for n in range(1, NK):
                        value = jnp.where(circle == n, phonons_ref[side, d, n, w], value)
                    hit = delta == (offset if side == 0 else -offset)
                    total = total + jnp.where(hit, value, 0.0)
            top = total.astype(jnp.bfloat16).astype(jnp.float32)
            blocks.append(jnp.where(fine, total - top, top))
        blocks.append(jnp.zeros(shape, jnp.float32))
        lhs_ref[pl.ds(k * GROUP, GROUP), :] = jnp.concatenate(blocks, axis=0).astype(jnp.bfloat16)


def left_products(picked, left_ref, half_ref, d, k, start, lanes):
    for p in range(half_ref.shape[2]):
        total = None
        for i in range(ORB):
            term = left_ref[i, d, pl.ds(start + p, HW, stride=0), :] * picked[i]
            total = term if total is None else total + term
        half_ref[d, k, p, :, lanes] = total


def right_products(right_ref, half_ref, outs):
    for k, out_ref in enumerate(outs):

        def right_side(p, carry):
            sums = [None] * PAIRS
            for d in range(DIRS):
                plain = [half_ref[d, k, p, :, pl.ds(jj * 128, 128)] for jj in range(PAIRS)]
                swapped = [pltpu.roll(v, NA, 1) for v in plain]
                for q in range(PAIRS):
                    for jj in range(PAIRS):
                        straight = right_ref[d, jj, 0, pl.ds(q, HW, stride=0), :]
                        crossed = right_ref[d, jj, 1, pl.ds(q, HW, stride=0), :]
                        term = straight * plain[jj] + crossed * swapped[jj]
                        sums[q] = term if sums[q] is None else sums[q] + term
            for q in range(PAIRS):
                out_ref[p, :, pl.ds(q * 128, 128)] = sums[q]
            return carry

        lax.fori_loop(0, out_ref.shape[0], right_side, 0, unroll=UNROLL_RIGHT)


def mix_kernel(count, first, moms, *refs):
    sources = refs[:count]
    lhs_ref, left_ref, right_ref, pick_ref, *outs = refs[count:-2]
    mixed_ref, half_ref = refs[-2:]
    depth = count * HW
    rows = len(moms) * GROUP

    def mix(jj, slot):
        lanes = pl.ds(pl.multiple_of(jj * 128, 128), 128)
        weights = lhs_ref[pl.ds(moms[0] * GROUP, rows), first : first + 3 * depth]
        for i in range(0, ORB, 2):
            block = jnp.concatenate(
                [
                    jnp.concatenate([source[i + n, :, lanes] for source in sources], axis=0)
                    for n in range(2)
                ],
                axis=1,
            )
            top = block.astype(jnp.bfloat16)
            rest = (block - top.astype(jnp.float32)).astype(jnp.bfloat16)
            product = jnp.dot(
                weights,
                jnp.concatenate([top, rest, top], axis=0),
                preferred_element_type=jnp.float32,
            )
            for k in range(len(moms)):
                for d in range(DIRS):
                    at = k * GROUP + d * HW
                    total = product[at : at + HW]
                    mixed_ref[slot, i, k, d] = total[:, :128]
                    mixed_ref[slot, i + 1, k, d] = total[:, 128:]

    def left_side(jj, slot):
        lanes = pl.ds(pl.multiple_of(jj * 128, 128), 128)
        for d in range(DIRS):
            pick = pick_ref[pl.ds(d, HW, stride=0), :]
            for k in range(len(moms)):
                picked = [
                    jnp.take_along_axis(
                        mixed_ref[slot, i, k, d], pick, axis=1, mode="promise_in_bounds"
                    )
                    for i in range(ORB)
                ]
                left_products(picked, left_ref, half_ref, d, k, 0, lanes)

    mix(0, 0)

    def step(t, carry):
        mix(2 * t + 1, 1)
        left_side(2 * t, 0)
        mix(jnp.minimum(2 * t + 2, PAIRS - 1), 0)
        left_side(2 * t + 1, 1)
        return carry

    lax.fori_loop(0, PAIRS // 2, step, 0)
    right_products(right_ref, half_ref, outs)


def join_kernel(own_ref, far_ref, near_edge_ref, far_edge_ref, out_ref, staged_ref, sems):
    half = lax.axis_index("mom") // 2

    def flush(j):
        lanes = pl.ds(j * 128, 128)
        return pltpu.make_async_copy(staged_ref.at[j], out_ref.at[:, lanes], sems.at[j])

    for j in range(PAIRS):
        lanes = pl.ds(j * 128, 128)
        for part in range(2):

            @pl.when(half == part)
            def _():
                for p in range(ORB):
                    staged_ref[j, pl.ds(part * ORB + p, HW, stride=2 * ORB), :] = (
                        own_ref[p, :, lanes] + near_edge_ref[p, :, lanes]
                    )
                    staged_ref[j, pl.ds((1 - part) * ORB + p, HW, stride=2 * ORB), :] = (
                        far_ref[p, :, lanes] + far_edge_ref[p, :, lanes]
                    )

        flush(j).start()
    for j in range(PAIRS):
        flush(j).wait()


def send(x, energy_of, flip):
    energies = lax.axis_size("energy")
    moms = lax.axis_size("mom")
    pairs = []
    for m in range(moms):
        for e in range(energies):
            to = energy_of(e)
            if 0 <= to < energies:
                pairs.append((m * energies + e, (m ^ flip) * energies + to))
    return lax.ppermute(x, ("mom", "energy"), pairs)


def stay(e):
    return e


def beyond(e):
    return e - 2 if e % 2 == 0 else e + 2


def pair(e):
    return e ^ 1


VMEM = pl.BlockSpec(memory_space=pltpu.VMEM)
SMEM = pl.BlockSpec(memory_space=pltpu.SMEM)
HBM = pl.BlockSpec(memory_space=pltpu.MemorySpace.HBM)
STAGED = [pltpu.VMEM((PAIRS, HW * 2 * ORB, 128), jnp.float32), pltpu.SemaphoreType.DMA((PAIRS,))]
BLOCK = jax.ShapeDtypeStruct((ORB, HW, WIDTH), jnp.float32)


def mix_call(sources, tables, first, moms, orbitals):
    count = len(sources)
    outs = [jax.ShapeDtypeStruct((orbitals, HW, WIDTH), jnp.float32)] * len(moms)
    return pl.pallas_call(
        functools.partial(mix_kernel, count, first, moms),
        out_shape=tuple(outs),
        in_specs=[VMEM] * (count + 4),
        out_specs=(VMEM,) * len(outs),
        scratch_shapes=[
            pltpu.VMEM((2, ORB, len(moms), DIRS, HW, 128), jnp.float32),
            pltpu.VMEM((DIRS, len(moms), orbitals, HW, WIDTH), jnp.float32),
        ],
        compiler_params=PARAMS,
        name="mix",
    )(*sources, *tables)


def layer(green, gradients, neighbours, phonons, offsets):
    mine, other = pl.pallas_call(
        split_kernel,
        out_shape=(BLOCK, BLOCK),
        in_specs=[HBM],
        out_specs=(VMEM, VMEM),
        scratch_shapes=STAGED,
        compiler_params=PARAMS,
        name="split",
    )(pltpu.with_memory_space_constraint(green.reshape(HW * 2 * ORB, WIDTH), pltpu.MemorySpace.HBM))
    here_far = send(other, stay, 2)
    beyond_own = send(mine, beyond, 0)
    here_near = send(mine, stay, 1)
    tables = pl.pallas_call(
        prepare_kernel,
        out_shape=(
            jax.ShapeDtypeStruct((2 * GROUP, 384), jnp.bfloat16),
            jax.ShapeDtypeStruct((ORB, DIRS, 16, 128), jnp.float32),
            jax.ShapeDtypeStruct((DIRS, PAIRS, 2, 8, 128), jnp.float32),
            jax.ShapeDtypeStruct((8, 128), jnp.int32),
        ),
        in_specs=[SMEM, SMEM, VMEM, VMEM],
        out_specs=(VMEM,) * 4,
        scratch_shapes=[pltpu.VMEM((16, 128), jnp.float32)],
        compiler_params=PARAMS,
        name="prepare",
    )(phonons.transpose(0, 1, 3, 2), offsets, neighbours, gradients)
    here_far, *tables = lax.optimization_barrier((here_far, *tables))
    beyond_far = send(here_far, beyond, 0)
    here_last = send(here_far, stay, 1)
    here = [mine, here_near, here_far, here_last]
    (far,) = mix_call(here, tables, 256, (1,), ORB)
    _, beyond_own, beyond_far = lax.optimization_barrier((far, beyond_own, beyond_far))
    far = send(far, stay, 2)
    there = [beyond_own, send(beyond_own, stay, 1), beyond_far, send(beyond_far, stay, 1)]
    near_edge, far_edge = mix_call(here + there, tables, 0, (0, 1), ORB)
    near_sent = send(near_edge, pair, 0)
    edges = [near_sent, send(far_edge, pair, 2)]
    here[0], near_edge = lax.optimization_barrier((mine, near_edge))
    (own,) = mix_call(here, tables, 256, (0,), ORB)
    out = pl.pallas_call(
        join_kernel,
        out_shape=jax.ShapeDtypeStruct((HW * 2 * ORB, WIDTH), jnp.float32),
        in_specs=[VMEM] * 4,
        out_specs=HBM,
        scratch_shapes=STAGED,
        compiler_params=PARAMS,
        name="join",
    )(own, far, *edges)
    return out.reshape(green.shape)


def solution(mesh):
    placed = (P("energy", "mom", None, None), P(), P(), P(), P())
    return jax.shard_map(
        layer,
        mesh=mesh,
        in_specs=placed,
        out_specs=P("energy", "mom", None, None),
        check_vma=False,
    )
```
